32 devices in a mesh: grp: 2 (over y), seq: 4 (over z), zero: 4 (over x, core).
Axes of the slice: x: 2, y: 2, z: 4, core: 2. Of those that a mesh axis runs over, the one named last changes fastest.
Arguments:
- hidden: bfloat16 [8, 512, 1280], P(('grp', 'zero'), 'seq'), parts along dimension 0, may hold values from -6 to 6
- grad_out: bfloat16 [8, 512, 1280], P(('grp', 'zero'), 'seq'), parts along dimension 0, may hold values from -6 to 6
- w_proj: bfloat16 [1280, 148], P('zero'), may hold values from -0.15625 to 0.15625
- conv_w: bfloat16 [4, 1408], P(None, 'zero'), may hold values from -3 to 3
- a_log: float32 [20], replicated, may hold values from -8 to 1, as said below
- dt_bias: float32 [20], replicated, may hold values from -4.5 to -3
Outputs:
- output: bfloat16 [8, 512, 1280], P(('grp', 'zero'), 'seq'), parts along dimension 0
- grad_hidden: bfloat16 [8, 512, 1280], P(('grp', 'zero'), 'seq'), parts along dimension 0
- grad_proj: float32 [2560, 148], P(('grp', 'zero')), parts along dimension 0
- grad_conv: float32 [8, 1408], P('grp', 'zero'), parts along dimension 0
- grad_heads: float32 [4, 20], P('grp'), parts along dimension 0
The draws below stay inside these ranges and needn't reach their ends.
There are 2 independent parts, one for each index of `grp`. The reference program is written for one: setup_inputs(seed, part) draws one part's arguments, and reference() takes and returns one part's arrays. A program takes and returns all parts, laid end to end along the dimension named above; an argument that names none is the same for every part. Nothing has to cross between parts.
Inputs may be any that keep to these rules, and one draw needn't show every extreme that they name: `a_log`: the logarithms of the heads' decay rates.
All inputs are finite; a program needn't handle non-finite values.
Results may differ from the reference program's by a relative error of at most 0.017.
Values may be sent and summed in bfloat16 or wider, within the bound.
A program may use at most 192 MiB of HBM per device.

```python
import math
import jax
import jax.numpy as jnp
from jax import lax

WIDTH = 1280
STATE = 64
HEAD_DIM = 64
SPAN = 128
KERNEL = 4
HEADS = 20
SEQ_LEN = 512
SEQS = 4


def draw_a_log(key, part):
    picked = jax.random.uniform(jax.random.fold_in(key, 11), (HEADS,))
    slow_rates = jax.random.uniform(jax.random.fold_in(key, 12), (HEADS,), minval=math.log(10.0 / SEQ_LEN), maxval=math.log(40.0 / SEQ_LEN))
    fast_rates = jax.random.uniform(jax.random.fold_in(key, 13), (HEADS,), minval=math.log(0.6), maxval=math.log(2.0))
    share = 0.5
    return jnp.where(picked < share, slow_rates, fast_rates).astype(jnp.float32)


def spiked(values, key, source, target, blocks, factor):
    owner, partner = [(jnp.arange(values.shape[dim]) // (values.shape[dim] // blocks)).reshape([-1 if axis == dim else 1 for axis in range(values.ndim)]) for dim in (source, target)]
    chosen = jax.random.permutation(key, blocks)[partner]
    strong = (owner == chosen) | (owner == (partner + blocks // 2) % blocks)
    return jnp.where(strong, factor * values, values)


def block_levels(own_key, dims, shards, low, top_value):
    def one(axis_at, parts):
        draws = jax.random.uniform(jax.random.fold_in(jax.random.fold_in(own_key, 6), axis_at), (parts,), jnp.float32, low / len(shards), top_value / len(shards))
        return jnp.repeat(jnp.exp(draws), dims[axis_at] // parts).reshape((-1,) + (1,) * (len(dims) - axis_at - 1))

    factor_of = one(*shards[0])
    for cut in shards[1:]:
        factor_of = factor_of * one(*cut)
    return factor_of


def centred(own_key, shape, scale, most, cuts=(), dtype=jnp.bfloat16):
    array = scale * jax.random.normal(own_key, shape, jnp.float32)
    if cuts:
        array = array * block_levels(own_key, shape, cuts, -0.22, 0.18)
    return jnp.clip(array, -most, most).astype(dtype)


def bell_draw_with(own_key, extent, scale, bound, split, heavy, held_as=jnp.bfloat16):
    entries = scale * jax.random.normal(own_key, extent, jnp.float32)
    if split:
        entries = entries * block_levels(own_key, extent, split, -0.22, 0.18)
    return jnp.clip(spiked(entries, jax.random.fold_in(own_key, 3), *heavy), -bound, bound).astype(held_as)


def setup_inputs(seed: int = 0, part: int = 0) -> dict:
    key_of = jax.random.split(jax.random.key(seed), 7)
    part_keys = jax.random.split(jax.random.fold_in(key_of[6], part), 7)
    return {
        "hidden": bell_draw_with(part_keys[0], (SEQS, SEQ_LEN, WIDTH), 1.0, 6.0, ((0, 4), (1, 4)), (0, 2, 4, 2.0)),
        "grad_out": centred(part_keys[1], (SEQS, SEQ_LEN, WIDTH), 1.0, 6.0, ((0, 4), (1, 4))),
        "w_proj": centred(key_of[2], (WIDTH, 2 * STATE + HEADS), WIDTH ** -0.5, 0.15625, ((0, 4),)),
        "conv_w": centred(key_of[3], (KERNEL, WIDTH + 2 * STATE), KERNEL ** -0.5, 3.0, ((1, 4),)),
        "a_log": draw_a_log(jax.random.fold_in(key_of[6], 71), part),
        "dt_bias": jnp.clip(jax.random.uniform(key_of[5], (HEADS,), jnp.float32, -4.5, -3.0), -4.5, -3.0),
    }


def conv_core(ahead_in, dt_raw, filters, a_log, dt_bias):
    length = dt_raw.shape[0]
    head_count = dt_raw.shape[1]
    blocks = length // SPAN
    mixed_sum = filters[0] * ahead_in[KERNEL - 1:KERNEL - 1 + length]
    for step_back in range(1, KERNEL):
        mixed_sum = mixed_sum + filters[step_back] * ahead_in[KERNEL - 1 - step_back:KERNEL - 1 - step_back + length]
    active = jax.nn.silu(mixed_sum)
    values = active[:, :WIDTH].astype(jnp.bfloat16).reshape(blocks, SPAN, head_count, HEAD_DIM)
    b_mat = active[:, WIDTH:WIDTH + STATE].astype(jnp.bfloat16).reshape(blocks, SPAN, STATE)
    c_mat = active[:, WIDTH + STATE:].astype(jnp.bfloat16)
    c_blocks = c_mat.reshape(blocks, SPAN, STATE)
    steps_dt = jax.nn.softplus(dt_raw + dt_bias)
    log_decay = -jnp.exp(a_log) * steps_dt
    within = jnp.cumsum(log_decay.reshape(blocks, SPAN, head_count), axis=1).transpose(0, 2, 1)
    dt_blocks = steps_dt.reshape(blocks, SPAN, head_count).transpose(0, 2, 1)
    scores = jnp.einsum('kin,kjn->kij', c_blocks.astype(jnp.float32), b_mat.astype(jnp.float32))
    causal = jnp.arange(SPAN)[:, None] >= jnp.arange(SPAN)[None, :]
    gap_log = within[:, :, :, None] - within[:, :, None, :]
    decays = jnp.exp(jnp.where(causal, gap_log, -jnp.inf))
    weights = (scores[:, None] * decays * dt_blocks[:, :, None, :]).astype(jnp.bfloat16)
    y_intra = jnp.einsum('khij,kjhp->kihp', weights.astype(jnp.float32), values.astype(jnp.float32))
    to_end = jnp.exp(within[:, :, -1:] - within) * dt_blocks
    b_weighted = (to_end[..., None] * b_mat[:, None, :, :].astype(jnp.float32)).astype(jnp.bfloat16)
    states = jnp.einsum('khjn,kjhp->khnp', b_weighted.astype(jnp.float32), values.astype(jnp.float32))
    totals = within[:, :, -1]

    def advance(carried, current):
        return (jnp.exp(current[0])[:, None, None] * carried + current[1], carried)
    last_state, entering = lax.scan(advance, jnp.zeros(states.shape[1:], jnp.float32), (totals, states))
    y_inter = jnp.einsum('kin,khnp->kihp', c_blocks.astype(jnp.float32), entering, precision=lax.Precision.HIGHEST)
    y_inter = y_inter * jnp.exp(within).transpose(0, 2, 1)[..., None]
    return (y_intra + y_inter).reshape(length, WIDTH)

def strand(tokens, cotangent, w_proj, filters, a_log, dt_bias):
    projected = jnp.dot(tokens, w_proj, preferred_element_type=jnp.float32)
    inner_act = jnp.concatenate([tokens, projected[:, :2 * STATE].astype(jnp.bfloat16)], axis=1)
    dt_raw = projected[:, 2 * STATE:]
    margin = KERNEL - 1

    def both_ways(inner_f32, dt_vals, filt, decay_log, bias):
        ahead_in = jnp.pad(inner_f32, ((margin, 0), (0, 0)))
        behind = jnp.pad(jnp.flip(inner_f32, axis=0), ((margin, 0), (0, 0)))
        y_ahead = conv_core(ahead_in, dt_vals, filt, decay_log, bias)
        y_behind = conv_core(behind, jnp.flip(dt_vals, axis=0), filt, decay_log, bias)
        return y_ahead + jnp.flip(y_behind, axis=0)
    total, pullback = jax.vjp(both_ways, inner_act.astype(jnp.float32), dt_raw, filters, a_log, dt_bias)
    result = total.astype(jnp.bfloat16)
    grad_inner32, grad_dt, grad_filt, grad_alog, grad_bias = pullback(cotangent.astype(jnp.float32))
    grad_inner = grad_inner32.astype(jnp.bfloat16)
    grad_projected = jnp.concatenate([grad_inner[:, WIDTH:], grad_dt.astype(jnp.bfloat16)], axis=1)
    grad_weight = jnp.dot(tokens.T, grad_projected, preferred_element_type=jnp.float32)
    grad_tokens = (grad_inner[:, :WIDTH].astype(jnp.float32) + jnp.dot(grad_projected, w_proj.T, preferred_element_type=jnp.float32)).astype(jnp.bfloat16)
    return (result, grad_tokens, grad_weight, grad_filt, jnp.stack([grad_alog, grad_bias]))

def reference(hidden, grad_out, w_proj, conv_w, a_log, dt_bias):
    filters = conv_w.astype(jnp.float32)

    def one_sequence(pieces):
        tokens, cotangent = pieces
        first = strand(tokens, cotangent, w_proj, filters, a_log, dt_bias)
        second = strand(jnp.flip(tokens, axis=1), jnp.flip(cotangent, axis=1), w_proj, filters, a_log, dt_bias)
        merged = (first[0].astype(jnp.float32) + jnp.flip(second[0], axis=1).astype(jnp.float32)).astype(jnp.bfloat16)
        grad_tok = (first[1].astype(jnp.float32) + jnp.flip(second[1], axis=1).astype(jnp.float32)).astype(jnp.bfloat16)
        return (merged, grad_tok, first[2] + second[2], first[3] + second[3], first[4] + second[4])
    outs = lax.map(one_sequence, (hidden, grad_out))
    return (outs[0], outs[1], lax.optimization_barrier(jnp.sum(outs[2], axis=0)), lax.optimization_barrier(jnp.sum(outs[3], axis=0)), lax.optimization_barrier(jnp.sum(outs[4], axis=0)))
```

```python
import functools
import jax
import jax.numpy as jnp
from jax import lax
from jax.experimental import pallas as pl
from jax.experimental.pallas import tpu as pltpu
from jax.sharding import PartitionSpec as P

WIDTH = 1280
STATE = 64
HEAD_DIM = 64
SPAN = 128
KERNEL = 4
HEADS = 20
PAIRS = WIDTH // 128
CHANNELS = WIDTH + 2 * STATE
EDGE = 8
EXT = SPAN + 2 * EDGE
F32 = jnp.float32
BF16 = jnp.bfloat16
LOW = -1e30
COMBOS = ((0, 0), (0, 1), (1, 0), (1, 1))


def mm(a, b):
    return jnp.dot(a, b, preferred_element_type=F32)


def mm_nt(a, b):
    return lax.dot_general(a, b, (((1,), (1,)), ((), ())), preferred_element_type=F32)


def mm_tn(a, b):
    return lax.dot_general(a, b, (((0,), (0,)), ((), ())), preferred_element_type=F32)


def exact(a, b):
    return jnp.dot(a, b, preferred_element_type=F32, precision=lax.Precision.HIGHEST)


def iota(dim, shape=(128, 128)):
    return lax.broadcasted_iota(jnp.int32, shape, dim)


def mirror(dtype=BF16):
    return jnp.where(iota(0) + iota(1) == 127, 1.0, 0.0).astype(dtype)


def col(x, h):
    return jnp.sum(jnp.where(iota(1) == h, x, 0.0), axis=1, keepdims=True)


def softplus(x):
    return jnp.maximum(x, 0.0) + jnp.log1p(jnp.exp(-jnp.abs(x)))


def sigmoid(x):
    return 1.0 / (1.0 + jnp.exp(-x))


def head_of(strand, pair, r):
    return 2 * pair + r if strand == 0 else HEADS - 1 - 2 * pair - r


def shifted(x):
    back = [x[EDGE : EDGE + SPAN]]
    fore = [back[0]]
    for k in range(1, KERNEL):
        back.append(pltpu.roll(x, k, 0)[EDGE : EDGE + SPAN])
        fore.append(pltpu.roll(x, EXT - k, 0)[EDGE : EDGE + SPAN])
    return back, fore


def conv(taps, rows):
    out = taps[0:1] * rows[0]
    for k in range(1, KERNEL):
        out = out + taps[k : k + 1] * rows[k]
    return out


def conv_back(taps, dm, direction):
    zero = jnp.zeros((EDGE, 128), F32)
    wide = jnp.concatenate([zero, dm, zero], axis=0)
    out = taps[0:1] * wide
    for k in range(1, KERNEL):
        out = out + taps[k : k + 1] * pltpu.roll(wide, EXT - k if direction == 0 else k, 0)
    return out


def tap_grads(dm, rows):
    parts = [jnp.sum(dm * rows[k], axis=0, keepdims=True) for k in range(KERNEL)]
    return jnp.concatenate(parts + [jnp.zeros((8 - KERNEL, 128), F32)], axis=0)


def last_row(x, direction):
    return x[SPAN - 1 : SPAN] if direction == 0 else x[0:1]


def lanes(i):
    return pl.ds(pl.multiple_of(i * 128, 128), 128)


def first_kernel(
    x_ref, go_ref, w_ref, f_ref, alog_ref, bias_ref,
    state_ref, gstate_ref, dec_ref, wr_ref, bcx_ref, dtx_ref, within_ref,
    tow_t, e_col, bc_t,
):
    flip = mirror()
    for b in range(PAIRS):
        wr_ref[b * 128 : (b + 1) * 128] = mm(
            flip, w_ref[(PAIRS - 1 - b) * 128 : (PAIRS - b) * 128]
        ).astype(BF16)
    x_all = x_ref[...]
    rate = jnp.exp(alog_ref[...])
    for s in range(2):
        proj = mm(x_all, w_ref[...] if s == 0 else wr_ref[...])
        bcx = proj[:, :128].astype(BF16).astype(F32)
        bcx_ref[s] = bcx
        dtx = proj[EDGE : EDGE + SPAN, 128:] + bias_ref[...]
        dtx_ref[s] = dtx
        delta = softplus(dtx)
        rows = shifted(bcx)
        for d in range(2):
            c = 2 * s + d
            tri = iota(0) >= iota(1) if d == 0 else iota(0) <= iota(1)
            within = exact(jnp.where(tri, 1.0, 0.0), -rate * delta)
            within_ref[c] = within
            mixed = conv(f_ref[:, WIDTH:], rows[d])
            act = (mixed * sigmoid(mixed)).astype(BF16).astype(F32)
            bc_t[c] = act.T
            tow_t[c] = (jnp.exp(last_row(within, d) - within) * delta).T
            e_col[c] = jnp.exp(within)
            dec_ref[c] = jnp.zeros((16, 128), F32)

    def pair_step(i, carry):
        x = x_ref[:, lanes(i)].astype(F32)
        g = go_ref[:, lanes(i)].astype(F32)
        rows = shifted(x)
        taps = (
            f_ref[:, lanes(i)],
            mm(f_ref[:, lanes(PAIRS - 1 - i)].astype(BF16), flip),
        )
        low = iota(1) < HEAD_DIM
        low_half = iota(1, (STATE, 128)) < HEAD_DIM
        for s, d in COMBOS:
            c = 2 * s + d
            mixed = conv(taps[s], rows[d])
            values = (mixed * sigmoid(mixed)).astype(BF16)
            heads = [head_of(s, i, r) for r in range(2)]
            b_t = bc_t[c, 0:STATE]
            bw = jnp.concatenate(
                [b_t * tow_t[c, pl.ds(h, 1), :] for h in heads], axis=0
            ).astype(BF16)
            st = mm(bw, values)
            state_ref[c, i] = jnp.where(low_half, st[:STATE], st[STATE:])
            e = e_col[c]
            e0, e1 = [col(e, h) for h in heads]
            e_pair = jnp.where(low, e0, e1)
            gstate_ref[c, i] = mm(bc_t[c, STATE:128].astype(BF16), (e_pair * g).astype(BF16))
            dec_ref[c, pl.ds(i, 1), :] = last_row(e_pair, d)
        return carry

    lax.fori_loop(0, PAIRS, pair_step, 0)


def main_kernel(
    x_ref, go_ref, f_ref, alog_ref, bcx_ref, dtx_ref, within_ref, sin_ref, gin_ref,
    out_ref, gi_ref, gf_ref, ddt_ref, heads_ref,
    e_col, f_col, tow, within_t, delta_t, score, d_score, d_b, d_c, d_l, d_lt, d_dc, d_dt, bc_act,
):
    flip = mirror()
    rate = jnp.exp(alog_ref[...])
    for s in range(2):
        delta = softplus(dtx_ref[s])
        delta_t[s] = delta.T
        rows = shifted(bcx_ref[s])
        d_dc[s] = jnp.zeros((128, 128), F32)
        d_dt[s] = jnp.zeros((128, 128), F32)
        for d in range(2):
            c = 2 * s + d
            within = within_ref[c]
            within_t[c] = within.T
            e_col[c] = jnp.exp(within)
            f = jnp.exp(last_row(within, d) - within)
            f_col[c] = f
            tow[c] = f * delta
            mixed = conv(f_ref[:, WIDTH:], rows[d])
            act = (mixed * sigmoid(mixed)).astype(BF16)
            bc_act[c, 0] = act[:, :STATE].astype(F32)
            bc_act[c, 1] = act[:, STATE:].astype(F32)
            score[c] = mm_nt(act[:, STATE:], act[:, :STATE])
            d_score[c] = jnp.zeros((128, 128), F32)
            d_l[c] = jnp.zeros((128, 128), F32)
            d_lt[c] = jnp.zeros((128, 128), F32)
            d_b[c] = jnp.zeros((128, STATE), F32)
            d_c[c] = jnp.zeros((128, STATE), F32)

    def pair_step(i, carry):
        x = x_ref[:, lanes(i)].astype(F32)
        go = go_ref[:, lanes(i)]
        g = go.astype(F32)
        rows = shifted(x)
        taps = (
            f_ref[:, lanes(i)],
            mm(f_ref[:, lanes(PAIRS - 1 - i)].astype(BF16), flip),
        )
        lane = iota(1)
        low = lane < HEAD_DIM
        low_half = iota(1, (STATE, 128)) < HEAD_DIM
        none = jnp.zeros((128, 128), BF16)
        g_two = jnp.concatenate([jnp.where(low, go, none), jnp.where(low, none, go)], axis=0)
        strands = []
        for s in range(2):
            y = jnp.zeros((128, 128), F32)
            gi = jnp.zeros((EXT, 128), F32)
            gf = jnp.zeros((8, 128), F32)
            heads = [head_of(s, i, r) for r in range(2)]
            delta_r = [delta_t[s, pl.ds(h, 1), :] for h in heads]
            for d in range(2):
                c = 2 * s + d
                end = SPAN - 1 if d == 0 else 0
                keep = iota(0) >= lane if d == 0 else iota(0) <= lane
                mixed = conv(taps[s], rows[d])
                sig = sigmoid(mixed)
                values = (mixed * sig).astype(BF16)
                b_mat, c_mat = bc_act[c, 0], bc_act[c, 1]
                within = within_ref[c]
                e_all, f_all, tow_all = e_col[c], f_col[c], tow[c]
                sc = score[c]
                decays, sds, ws, tows, fs, es = [], [], [], [], [], []
                for r, h in enumerate(heads):
                    gap = jnp.where(keep, col(within, h) - within_t[c, pl.ds(h, 1), :], LOW)
                    decay = jnp.exp(gap)
                    decays.append(decay)
                    sds.append(sc * decay)
                    ws.append((sds[r] * delta_r[r]).astype(BF16))
                    tows.append(col(tow_all, h))
                    fs.append(col(f_all, h))
                    es.append(col(e_all, h))
                e_pair = jnp.where(low, es[0], es[1])
                ge = (e_pair * g).astype(BF16)
                s_in, g_in = sin_ref[c, i], gin_ref[c, i]
                y_two = mm(jnp.concatenate(ws, axis=0), values)
                inter = mm(c_mat.astype(BF16), s_in) * e_pair
                y = y + jnp.where(low, y_two[:128], y_two[128:]) + inter
                d_w = mm_nt(g_two, values)
                bws = jnp.concatenate([(t * b_mat).astype(BF16) for t in tows], axis=0)
                dv_state = mm(bws, g_in)
                dv = jnp.where(
                    low,
                    mm_tn(ws[0], go) + dv_state[:128],
                    mm_tn(ws[1], go) + dv_state[128:],
                )
                v_two = jnp.concatenate(
                    [jnp.where(low, values, none), jnp.where(low, none, values)], axis=0
                )
                d_bw = mm_nt(v_two, g_in)
                d_c[c] += mm_nt(ge, s_in)
                q = g * inter
                both = jnp.sum(g_in.astype(F32) * s_in.astype(F32), axis=0, keepdims=True)
                ends = both * last_row(e_pair, d)
                low_row = iota(1, (1, 128)) < HEAD_DIM
                ds = d_score[c]
                db = d_b[c]
                dl = d_l[c]
                dd = d_dc[s]
                for r, h in enumerate(heads):
                    mine = low if r == 0 else ~low
                    mine_row = low_row if r == 0 else ~low_row
                    dw = d_w[128 * r : 128 * r + 128]
                    rr = dw * sds[r]
                    rows_sum = jnp.sum(rr * delta_r[r], axis=1, keepdims=True)
                    cols_sum = jnp.sum(rr, axis=0, keepdims=True)
                    d_dt[s, pl.ds(h, 1), :] += cols_sum
                    d_lt[c, pl.ds(h, 1), :] -= cols_sum * delta_r[r]
                    ds = ds + dw * decays[r] * delta_r[r]
                    dbw = d_bw[128 * r : 128 * r + 128]
                    d_tow = jnp.sum(dbw * b_mat, axis=1, keepdims=True)
                    db = db + tows[r] * dbw
                    dd = dd + jnp.where(lane == h, d_tow * fs[r], 0.0)
                    t = d_tow * tows[r]
                    total = jnp.sum(t, axis=0, keepdims=True) + jnp.sum(
                        jnp.where(mine_row, ends, 0.0), axis=1, keepdims=True
                    )
                    q_sum = jnp.sum(jnp.where(mine, q, 0.0), axis=1, keepdims=True)
                    at_end = jnp.where(iota(0, (128, 1)) == end, total, 0.0)
                    dl = dl + jnp.where(lane == h, rows_sum - t + q_sum + at_end, 0.0)
                d_score[c] = ds
                d_b[c] = db
                d_l[c] = dl
                d_dc[s] = dd
                dact = dv.astype(BF16).astype(F32)
                dm = dact * (sig * (1.0 + mixed * (1.0 - sig)))
                gf = gf + tap_grads(dm, rows[d])
                gi = gi + conv_back(taps[s], dm, d)
            strands.append(y.astype(BF16).astype(F32))
            gi_ref[s, :, lanes(i)] = gi
            gf_ref[s, :, lanes(i)] = gf
        out_ref[:, lanes(i)] = (strands[0] + strands[1]).astype(BF16)
        return carry

    lax.fori_loop(0, PAIRS, pair_step, 0)

    d_alog = jnp.zeros((1, 128), F32)
    d_bias = jnp.zeros((1, 128), F32)
    for s in range(2):
        rows = shifted(bcx_ref[s])
        dtx = dtx_ref[s]
        log_decay = -rate * softplus(dtx)
        d_delta = d_dc[s] + d_dt[s].T
        gi = jnp.zeros((EXT, 128), F32)
        gf = jnp.zeros((8, 128), F32)
        taps = f_ref[:, WIDTH:]
        for d in range(2):
            c = 2 * s + d
            tri = iota(0) <= iota(1) if d == 0 else iota(0) >= iota(1)
            d_log = exact(jnp.where(tri, 1.0, 0.0), d_l[c] + d_lt[c].T)
            d_delta = d_delta - rate * d_log
            d_alog = d_alog + jnp.sum(d_log * log_decay, axis=0, keepdims=True)
            ds = d_score[c].astype(BF16)
            dc = d_c[c] + mm(ds, bc_act[c, 0].astype(BF16))
            db = d_b[c] + mm_tn(ds, bc_act[c, 1].astype(BF16))
            dact = jnp.concatenate([db, dc], axis=1).astype(BF16).astype(F32)
            mixed = conv(taps, rows[d])
            sig = sigmoid(mixed)
            dm = dact * (sig * (1.0 + mixed * (1.0 - sig)))
            gf = gf + tap_grads(dm, rows[d])
            gi = gi + conv_back(taps, dm, d)
        d_raw = d_delta * sigmoid(dtx)
        ddt_ref[s] = d_raw.astype(BF16)
        d_bias = d_bias + jnp.sum(d_raw, axis=0, keepdims=True)
        gi_ref[s, :, WIDTH:] = gi
        gf_ref[s, :, WIDTH:] = gf
    heads_ref[...] = jnp.concatenate([d_alog, d_bias, jnp.zeros((6, 128), F32)], axis=0)


def last_kernel(
    hid_ref, w_ref, wr_ref, gi_ref, before_ref, after_ref, ddt_ref, gf_ref,
    gh_ref, gw_ref, gc_ref,
):
    flip = mirror()

    def own(s, at):
        top = gi_ref[s, EDGE : 2 * EDGE, at] + before_ref[s, :, at].astype(F32)
        low = gi_ref[s, SPAN : SPAN + EDGE, at] + after_ref[s, :, at].astype(F32)
        return jnp.concatenate([top, gi_ref[s, 2 * EDGE : SPAN, at], low], axis=0).astype(BF16)

    gps = [
        jnp.concatenate([own(s, slice(WIDTH, CHANNELS)), ddt_ref[s]], axis=1) for s in range(2)
    ]
    for i in range(PAIRS):
        at = slice(i * 128, i * 128 + 128)
        other = slice((PAIRS - 1 - i) * 128, (PAIRS - i) * 128)
        hid_flip = mm(hid_ref[:, other], flip).astype(BF16)
        gw_ref[at] = (mm_tn(hid_ref[:, at], gps[0]) + mm_tn(hid_flip, gps[1])).astype(gw_ref.dtype)
        a = (own(0, at).astype(F32) + mm_nt(gps[0], w_ref[at])).astype(BF16)
        b = (own(1, at).astype(F32) + mm_nt(gps[1], wr_ref[at])).astype(BF16)
        gh_ref[:, at] = (a.astype(F32) + b.astype(F32)).astype(BF16)
        gc_ref[:, at] = gf_ref[0, :, at] + exact(gf_ref[1, :, other], mirror(F32))
    gc_ref[:, WIDTH:] = gf_ref[0, :, WIDTH:] + gf_ref[1, :, WIDTH:]


def call(body, outs, scratch=()):
    return pl.pallas_call(
        body,
        out_shape=[jax.ShapeDtypeStruct(s, t) for s, t in outs],
        scratch_shapes=[pltpu.VMEM(s, F32) for s in scratch],
        compiler_params=pltpu.CompilerParams(vmem_limit_bytes=48 * 1024 * 1024),
    )


SQ4 = (4, 128, 128)
SQ2 = (2, 128, 128)


def per_device(hidden, grad_out, w_proj, conv_w, a_log, dt_bias):
    hid, go = hidden[0], grad_out[0]
    assert hidden.shape[:2] == (1, SPAN)
    size = lax.axis_size("seq")
    up = [(i, i + 1) for i in range(size - 1)]
    down = [(i + 1, i) for i in range(size - 1)]
    before = lax.ppermute(hid[SPAN - EDGE :], "seq", up)
    after = lax.ppermute(hid[:EDGE], "seq", down)
    x_ext = jnp.concatenate([before, hid, after], axis=0)
    w_pad = jnp.pad(w_proj, ((0, 0), (0, 256 - w_proj.shape[1])))
    w_full = lax.all_gather(w_pad, "zero", axis=0, tiled=True)
    conv_full = lax.all_gather(conv_w, "zero", axis=1, tiled=True)
    filters = jnp.pad(conv_full.astype(F32), ((0, 8 - KERNEL), (0, 0)))
    alog = jnp.pad(a_log, (0, 128 - HEADS))[None]
    bias = jnp.pad(dt_bias, (0, 128 - HEADS))[None]
    pieces = (4, PAIRS, STATE, 128)
    state, gstate, dec, w_rev, bcx, dtx, within = call(
        first_kernel,
        [
            (pieces, F32), (pieces, F32), ((4, 16, 128), F32), ((WIDTH, 256), BF16),
            ((2, EXT, 128), F32), (SQ2, F32), (SQ4, F32),
        ],
        [SQ4, SQ4, SQ4],
    )(x_ext, go, w_full, filters, alog, bias)
    dec = dec[:, :PAIRS, None, :]
    own_up = jnp.stack([state[0], state[2], gstate[1], gstate[3]])
    own_down = jnp.stack([state[1], state[3], gstate[0], gstate[2]])
    dec_up = jnp.stack([dec[0], dec[2], dec[1], dec[3]])
    dec_down = jnp.stack([dec[1], dec[3], dec[0], dec[2]])
    in_up = in_down = None
    for hop in range(size - 1):
        out_up, out_down = own_up, own_down
        if hop:
            out_up = own_up + dec_up * in_up.astype(F32)
            out_down = own_down + dec_down * in_down.astype(F32)
        in_up = lax.ppermute(out_up.astype(BF16), "seq", up)
        in_down = lax.ppermute(out_down.astype(BF16), "seq", down)
    s_in = jnp.stack([in_up[0], in_down[0], in_up[1], in_down[1]])
    g_in = jnp.stack([in_down[2], in_up[2], in_down[3], in_up[3]])
    output, gi, gf, ddt, heads = call(
        main_kernel,
        [
            ((SPAN, WIDTH), BF16), ((2, EXT, CHANNELS), F32), ((2, 8, CHANNELS), F32),
            (SQ2, BF16), ((8, 128), F32),
        ],
        [
            SQ4, SQ4, SQ4, SQ4, SQ2, SQ4, SQ4, (4, 128, STATE), (4, 128, STATE), SQ4, SQ4,
            SQ2, SQ2, (4, 2, 128, STATE),
        ],
    )(x_ext, go, filters, alog, bcx, dtx, within, s_in, g_in)
    rim_before = lax.ppermute(gi[:, EDGE + SPAN :].astype(BF16), "seq", up)
    rim_after = lax.ppermute(gi[:, :EDGE].astype(BF16), "seq", down)
    grad_hidden, gw, gc = call(
        last_kernel,
        [((SPAN, WIDTH), BF16), ((WIDTH, 256), F32), ((8, CHANNELS), F32)],
    )(hid, w_full, w_rev, gi, rim_before, rim_after, ddt, gf)
    gw = gw[:, : w_proj.shape[1]].astype(BF16)
    part_w = lax.psum_scatter(gw, "zero", scatter_dimension=0, tiled=True)
    part_c = lax.psum_scatter(gc[:KERNEL].astype(BF16), "zero", scatter_dimension=1, tiled=True)
    share_w, share_c = lax.psum((part_w, part_c), "seq")
    grad_heads = lax.psum(heads[:2, :HEADS], ("seq", "zero"))
    return (output[None], grad_hidden[None], share_w.astype(F32), share_c.astype(F32), grad_heads)


def solution(mesh):
    return jax.shard_map(
        per_device,
        mesh=mesh,
        in_specs=(
            P(("grp", "zero"), "seq", None),
            P(("grp", "zero"), "seq", None),
            P("zero", None),
            P(None, "zero"),
            P(),
            P(),
        ),
        out_specs=(
            P(("grp", "zero"), "seq", None),
            P(("grp", "zero"), "seq", None),
            P(("grp", "zero"), None),
            P("grp", "zero"),
            P("grp", None),
        ),
        check_vma=False,
    )
```

```python
import functools
import jax
import jax.numpy as jnp
from jax import lax
from jax.experimental import pallas as pl
from jax.experimental.pallas import tpu as pltpu
from jax.sharding import PartitionSpec as P

WIDTH = 1280
STATE = 64
HEAD_DIM = 64
SPAN = 128
KERNEL = 4
HEADS = 20
PAIRS = WIDTH // 128
CHANNELS = WIDTH + 2 * STATE
EDGE = 8
EXT = SPAN + 2 * EDGE
F32 = jnp.float32
BF16 = jnp.bfloat16
LOW = -1e30
COMBOS = ((0, 0), (0, 1), (1, 0), (1, 1))


def mm(a, b):
    return jnp.dot(a, b, preferred_element_type=F32)


def mm_nt(a, b):
    return lax.dot_general(a, b, (((1,), (1,)), ((), ())), preferred_element_type=F32)


def mm_tn(a, b):
    return lax.dot_general(a, b, (((0,), (0,)), ((), ())), preferred_element_type=F32)


def exact(a, b):
    return jnp.dot(a, b, preferred_element_type=F32, precision=lax.Precision.HIGHEST)


def iota(dim, shape=(128, 128)):
    return lax.broadcasted_iota(jnp.int32, shape, dim)


def mirror(dtype=BF16):
    return jnp.where(iota(0) + iota(1) == 127, 1.0, 0.0).astype(dtype)


def col(x, h):
    return jnp.sum(jnp.where(iota(1) == h, x, 0.0), axis=1, keepdims=True)


def softplus(x):
    return jnp.maximum(x, 0.0) + jnp.log1p(jnp.exp(-jnp.abs(x)))


def sigmoid(x):
    return 1.0 / (1.0 + jnp.exp(-x))


def head_of(strand, pair, r):
    return 2 * pair + r if strand == 0 else HEADS - 1 - 2 * pair - r


def shifted(x):
    back = [x[EDGE : EDGE + SPAN]]
    fore = [back[0]]
    for k in range(1, KERNEL):
        back.append(pltpu.roll(x, k, 0)[EDGE : EDGE + SPAN])
        fore.append(pltpu.roll(x, EXT - k, 0)[EDGE : EDGE + SPAN])
    return back, fore


def conv(taps, rows):
    out = taps[0:1] * rows[0]
    for k in range(1, KERNEL):
        out = out + taps[k : k + 1] * rows[k]
    return out


def conv_back(taps, dm, direction):
    zero = jnp.zeros((EDGE, 128), F32)
    wide = jnp.concatenate([zero, dm, zero], axis=0)
    out = taps[0:1] * wide
    for k in range(1, KERNEL):
        out = out + taps[k : k + 1] * pltpu.roll(wide, EXT - k if direction == 0 else k, 0)
    return out


def tap_grads(dm, rows):
    parts = [jnp.sum(dm * rows[k], axis=0, keepdims=True) for k in range(KERNEL)]
    return jnp.concatenate(parts + [jnp.zeros((8 - KERNEL, 128), F32)], axis=0)


def last_row(x, direction):
    return x[SPAN - 1 : SPAN] if direction == 0 else x[0:1]


def lanes(i):
    return pl.ds(pl.multiple_of(i * 128, 128), 128)


def first_kernel(
    x_ref, go_ref, w_ref, f_ref, alog_ref, bias_ref,
    up_ref, down_ref, dup_ref, ddown_ref, wr_ref, bcx_ref, dtx_ref, within_ref,
    tow_t, e_col, bc_t,
):
    flip = mirror()
    for b in range(PAIRS):
        wr_ref[b * 128 : (b + 1) * 128] = mm(
            flip, w_ref[(PAIRS - 1 - b) * 128 : (PAIRS - b) * 128]
        ).astype(BF16)
    x_all = x_ref[...]
    rate = jnp.exp(alog_ref[...])
    for s in range(2):
        proj = mm(x_all, w_ref[...] if s == 0 else wr_ref[...])
        bcx = proj[:, :128].astype(BF16).astype(F32)
        bcx_ref[s] = bcx
        dtx = proj[EDGE : EDGE + SPAN, 128:] + bias_ref[...]
        dtx_ref[s] = dtx
        delta = softplus(dtx)
        rows = shifted(bcx)
        for d in range(2):
            c = 2 * s + d
            tri = iota(0) >= iota(1) if d == 0 else iota(0) <= iota(1)
            within = exact(jnp.where(tri, 1.0, 0.0), -rate * delta)
            within_ref[c] = within
            mixed = conv(f_ref[:, WIDTH:], rows[d])
            act = (mixed * sigmoid(mixed)).astype(BF16).astype(F32)
            bc_t[c] = act.T
            tow_t[c] = (jnp.exp(last_row(within, d) - within) * delta).T
            e_col[c] = jnp.exp(within)

    own_refs = (up_ref, down_ref)
    dec_refs = (dup_ref, ddown_ref)

    def pair_step(i, carry):
        x = x_ref[:, lanes(i)].astype(F32)
        g = go_ref[:, lanes(i)].astype(F32)
        rows = shifted(x)
        taps = (
            f_ref[:, lanes(i)],
            mm(f_ref[:, lanes(PAIRS - 1 - i)].astype(BF16), flip),
        )
        low = iota(1) < HEAD_DIM
        low_half = iota(1, (STATE, 128)) < HEAD_DIM
        for s, d in COMBOS:
            c = 2 * s + d
            mixed = conv(taps[s], rows[d])
            values = (mixed * sigmoid(mixed)).astype(BF16)
            heads = [head_of(s, i, r) for r in range(2)]
            b_t = bc_t[c, 0:STATE]
            bw = jnp.concatenate(
                [b_t * tow_t[c, pl.ds(h, 1), :] for h in heads], axis=0
            ).astype(BF16)
            st = mm(bw, values)
            own_refs[d][i, s] = jnp.where(low_half, st[:STATE], st[STATE:])
            e = e_col[c]
            e0, e1 = [col(e, h) for h in heads]
            e_pair = jnp.where(low, e0, e1)
            own_refs[1 - d][i, 2 + s] = mm(
                bc_t[c, STATE:128].astype(BF16), (e_pair * g).astype(BF16)
            )
            decay = jnp.broadcast_to(last_row(e_pair, d), (8, 128))
            dec_refs[d][i, s] = decay
            dec_refs[1 - d][i, 2 + s] = decay
        return carry

    lax.fori_loop(0, PAIRS, pair_step, 0)


def main_kernel(
    x_ref, go_ref, f_ref, alog_ref, bcx_ref, dtx_ref, within_ref, up_ref, down_ref,
    out_ref, gi_ref, gf_ref, ddt_ref, heads_ref,
    e_col, f_col, tow, within_t, delta_t, score, d_score, d_b, d_c, d_l, d_lt, d_dc, d_dt, bc_act,
):
    flip = mirror()
    rate = jnp.exp(alog_ref[...])
    for s in range(2):
        delta = softplus(dtx_ref[s])
        delta_t[s] = delta.T
        rows = shifted(bcx_ref[s])
        d_dc[s] = jnp.zeros((128, 128), F32)
        d_dt[s] = jnp.zeros((128, 128), F32)
        for d in range(2):
            c = 2 * s + d
            within = within_ref[c]
            within_t[c] = within.T
            e_col[c] = jnp.exp(within)
            f = jnp.exp(last_row(within, d) - within)
            f_col[c] = f
            tow[c] = f * delta
            mixed = conv(f_ref[:, WIDTH:], rows[d])
            act = (mixed * sigmoid(mixed)).astype(BF16)
            bc_act[c, 0] = act[:, :STATE].astype(F32)
            bc_act[c, 1] = act[:, STATE:].astype(F32)
            score[c] = mm_nt(act[:, STATE:], act[:, :STATE])
            d_score[c] = jnp.zeros((128, 128), F32)
            d_l[c] = jnp.zeros((128, 128), F32)
            d_lt[c] = jnp.zeros((128, 128), F32)
            d_b[c] = jnp.zeros((128, STATE), F32)
            d_c[c] = jnp.zeros((128, STATE), F32)

    def pair_step(i, carry):
        x = x_ref[:, lanes(i)].astype(F32)
        go = go_ref[:, lanes(i)]
        g = go.astype(F32)
        rows = shifted(x)
        taps = (
            f_ref[:, lanes(i)],
            mm(f_ref[:, lanes(PAIRS - 1 - i)].astype(BF16), flip),
        )
        lane = iota(1)
        low = lane < HEAD_DIM
        low_half = iota(1, (STATE, 128)) < HEAD_DIM
        none = jnp.zeros((128, 128), BF16)
        g_two = jnp.concatenate([jnp.where(low, go, none), jnp.where(low, none, go)], axis=0)
        strands = []
        for s in range(2):
            y = jnp.zeros((128, 128), F32)
            gi = jnp.zeros((EXT, 128), F32)
            gf = jnp.zeros((8, 128), F32)
            heads = [head_of(s, i, r) for r in range(2)]
            delta_r = [delta_t[s, pl.ds(h, 1), :] for h in heads]
            for d in range(2):
                c = 2 * s + d
                end = SPAN - 1 if d == 0 else 0
                keep = iota(0) >= lane if d == 0 else iota(0) <= lane
                mixed = conv(taps[s], rows[d])
                sig = sigmoid(mixed)
                values = (mixed * sig).astype(BF16)
                b_mat, c_mat = bc_act[c, 0], bc_act[c, 1]
                within = within_ref[c]
                e_all, f_all, tow_all = e_col[c], f_col[c], tow[c]
                sc = score[c]
                decays, sds, ws, tows, fs, es = [], [], [], [], [], []
                for r, h in enumerate(heads):
                    gap = jnp.where(keep, col(within, h) - within_t[c, pl.ds(h, 1), :], LOW)
                    decay = jnp.exp(gap)
                    decays.append(decay)
                    sds.append(sc * decay)
                    ws.append((sds[r] * delta_r[r]).astype(BF16))
                    tows.append(col(tow_all, h))
                    fs.append(col(f_all, h))
                    es.append(col(e_all, h))
                e_pair = jnp.where(low, es[0], es[1])
                ge = (e_pair * g).astype(BF16)
                ahead, behind = (up_ref, down_ref) if d == 0 else (down_ref, up_ref)
                s_in, g_in = ahead[i, s], behind[i, 2 + s]
                y_two = mm(jnp.concatenate(ws, axis=0), values)
                inter = mm(c_mat.astype(BF16), s_in) * e_pair
                y = y + jnp.where(low, y_two[:128], y_two[128:]) + inter
                d_w = mm_nt(g_two, values)
                bws = jnp.concatenate([(t * b_mat).astype(BF16) for t in tows], axis=0)
                dv_state = mm(bws, g_in)
                dv = jnp.where(
                    low,
                    mm_tn(ws[0], go) + dv_state[:128],
                    mm_tn(ws[1], go) + dv_state[128:],
                )
                v_two = jnp.concatenate(
                    [jnp.where(low, values, none), jnp.where(low, none, values)], axis=0
                )
                d_bw = mm_nt(v_two, g_in)
                d_c[c] += mm_nt(ge, s_in)
                q = g * inter
                both = jnp.sum(g_in.astype(F32) * s_in.astype(F32), axis=0, keepdims=True)
                ends = both * last_row(e_pair, d)
                low_row = iota(1, (1, 128)) < HEAD_DIM
                ds = d_score[c]
                db = d_b[c]
                dl = d_l[c]
                dd = d_dc[s]
                for r, h in enumerate(heads):
                    mine = low if r == 0 else ~low
                    mine_row = low_row if r == 0 else ~low_row
                    dw = d_w[128 * r : 128 * r + 128]
                    rr = dw * sds[r]
                    rows_sum = jnp.sum(rr * delta_r[r], axis=1, keepdims=True)
                    cols_sum = jnp.sum(rr, axis=0, keepdims=True)
                    d_dt[s, pl.ds(h, 1), :] += cols_sum
                    d_lt[c, pl.ds(h, 1), :] -= cols_sum * delta_r[r]
                    ds = ds + dw * decays[r] * delta_r[r]
                    dbw = d_bw[128 * r : 128 * r + 128]
                    d_tow = jnp.sum(dbw * b_mat, axis=1, keepdims=True)
                    db = db + tows[r] * dbw
                    dd = dd + jnp.where(lane == h, d_tow * fs[r], 0.0)
                    t = d_tow * tows[r]
                    total = jnp.sum(t, axis=0, keepdims=True) + jnp.sum(
                        jnp.where(mine_row, ends, 0.0), axis=1, keepdims=True
                    )
                    q_sum = jnp.sum(jnp.where(mine, q, 0.0), axis=1, keepdims=True)
                    at_end = jnp.where(iota(0, (128, 1)) == end, total, 0.0)
                    dl = dl + jnp.where(lane == h, rows_sum - t + q_sum + at_end, 0.0)
                d_score[c] = ds
                d_b[c] = db
                d_l[c] = dl
                d_dc[s] = dd
                dact = dv.astype(BF16).astype(F32)
                dm = dact * (sig * (1.0 + mixed * (1.0 - sig)))
                gf = gf + tap_grads(dm, rows[d])
                gi = gi + conv_back(taps[s], dm, d)
            strands.append(y.astype(BF16).astype(F32))
            gi_ref[s, :, lanes(i)] = gi
            gf_ref[s, :, lanes(i)] = gf
        out_ref[:, lanes(i)] = (strands[0] + strands[1]).astype(BF16)
        return carry

    lax.fori_loop(0, PAIRS, pair_step, 0)

    d_alog = jnp.zeros((1, 128), F32)
    d_bias = jnp.zeros((1, 128), F32)
    for s in range(2):
        rows = shifted(bcx_ref[s])
        dtx = dtx_ref[s]
        log_decay = -rate * softplus(dtx)
        d_delta = d_dc[s] + d_dt[s].T
        gi = jnp.zeros((EXT, 128), F32)
        gf = jnp.zeros((8, 128), F32)
        taps = f_ref[:, WIDTH:]
        for d in range(2):
            c = 2 * s + d
            tri = iota(0) <= iota(1) if d == 0 else iota(0) >= iota(1)
            d_log = exact(jnp.where(tri, 1.0, 0.0), d_l[c] + d_lt[c].T)
            d_delta = d_delta - rate * d_log
            d_alog = d_alog + jnp.sum(d_log * log_decay, axis=0, keepdims=True)
            ds = d_score[c].astype(BF16)
            dc = d_c[c] + mm(ds, bc_act[c, 0].astype(BF16))
            db = d_b[c] + mm_tn(ds, bc_act[c, 1].astype(BF16))
            dact = jnp.concatenate([db, dc], axis=1).astype(BF16).astype(F32)
            mixed = conv(taps, rows[d])
            sig = sigmoid(mixed)
            dm = dact * (sig * (1.0 + mixed * (1.0 - sig)))
            gf = gf + tap_grads(dm, rows[d])
            gi = gi + conv_back(taps, dm, d)
        d_raw = d_delta * sigmoid(dtx)
        ddt_ref[s] = d_raw.astype(BF16)
        d_bias = d_bias + jnp.sum(d_raw, axis=0, keepdims=True)
        gi_ref[s, :, WIDTH:] = gi
        gf_ref[s, :, WIDTH:] = gf
    heads_ref[...] = jnp.concatenate([d_alog, d_bias, jnp.zeros((6, 128), F32)], axis=0)


MESH = pl.DeviceIdType.MESH


def greet_all(sizes):
    barrier = pltpu.get_barrier_semaphore()
    for axis, size in sizes:
        me = lax.axis_index(axis)
        for k in range(1, size):
            pl.semaphore_signal(
                barrier, inc=1, device_id={axis: lax.rem(me + k, size)}, device_id_type=MESH
            )
    pl.semaphore_wait(barrier, sum(size - 1 for _, size in sizes))


def push(src, dst, send, recv, axis, peer):
    return pltpu.make_async_remote_copy(
        src_ref=src,
        dst_ref=dst,
        send_sem=send,
        recv_sem=recv,
        device_id={axis: peer},
        device_id_type=MESH,
    )


def greet_sides(me, count, more=0):
    barrier = pltpu.get_barrier_semaphore()
    for k in (1, count - 1):
        pl.semaphore_signal(
            barrier, inc=1, device_id={"seq": lax.rem(me + k, count)}, device_id_type=MESH
        )
    pl.semaphore_wait(barrier, 2 + more)


def gather_kernel(
    shards, count, hid_ref, w_ref, c_ref, x_ref, w_out, f_out,
    w_slots, c_own, c_slots, before, after, send, recv, sides,
):
    seq, zero = lax.axis_index("seq"), lax.axis_index("zero")
    barrier = pltpu.get_barrier_semaphore()
    for k in range(1, shards):
        pl.semaphore_signal(
            barrier, inc=1, device_id={"zero": lax.rem(zero + k, shards)}, device_id_type=MESH
        )
    greet_sides(seq, count, shards - 1)
    up = push(
        hid_ref.at[pl.ds(SPAN - 2 * EDGE, 2 * EDGE)], before, sides.at[0], sides.at[1], "seq",
        lax.rem(seq + 1, count),
    )
    down = push(
        hid_ref.at[pl.ds(0, 2 * EDGE)], after, sides.at[2], sides.at[3], "seq",
        lax.rem(seq + count - 1, count),
    )

    @pl.when(seq < count - 1)
    def _():
        up.start()

    @pl.when(seq > 0)
    def _():
        down.start()

    c_own[...] = jnp.zeros_like(c_own)
    c_own[:KERNEL] = c_ref[...].astype(F32)
    copies = []
    for k in range(1, shards):
        peer = lax.rem(zero + k, shards)
        copies.append(push(w_ref, w_slots.at[zero], send.at[k, 0], recv.at[k, 0], "zero", peer))
        copies.append(push(c_own, c_slots.at[zero], send.at[k, 1], recv.at[k, 1], "zero", peer))
    for copy in copies:
        copy.start()
    w_slots[zero] = w_ref[...]
    c_slots[zero] = c_own[...]
    w_out[:, 128:] = jnp.zeros((WIDTH, 128), BF16)
    x_ref[EDGE : EDGE + SPAN] = hid_ref[...]

    @pl.when(seq == 0)
    def _():
        x_ref[:EDGE] = jnp.zeros((EDGE, WIDTH), BF16)

    @pl.when(seq > 0)
    def _():
        up.wait_recv()
        x_ref[:EDGE] = before[EDGE:]

    @pl.when(seq == count - 1)
    def _():
        x_ref[EDGE + SPAN :] = jnp.zeros((EDGE, WIDTH), BF16)

    @pl.when(seq < count - 1)
    def _():
        down.wait_recv()
        x_ref[EDGE + SPAN :] = after[:EDGE]

    for copy in copies:
        copy.wait()
    rows, columns = w_ref.shape
    part = c_ref.shape[1]
    for z in range(shards):
        w_out[z * rows : (z + 1) * rows, :columns] = w_slots[z]
        f_out[:, z * part : (z + 1) * part] = c_slots[z]

    @pl.when(seq < count - 1)
    def _():
        up.wait_send()

    @pl.when(seq > 0)
    def _():
        down.wait_send()


def chain_kernel(
    count, own_up, own_down, dec_up, dec_down, in_up, in_down,
    out_up, out_down, send, recv,
):
    me = lax.axis_index("seq")
    greet_sides(me, count)

    @pl.when(me == 0)
    def _():
        in_up[...] = jnp.zeros_like(in_up)

    @pl.when(me == count - 1)
    def _():
        in_down[...] = jnp.zeros_like(in_down)

    ways = (
        (own_up, dec_up, in_up, out_up, me > 0, me < count - 1, lax.rem(me + 1, count)),
        (
            own_down, dec_down, in_down, out_down, me < count - 1, me > 0,
            lax.rem(me + count - 1, count),
        ),
    )
    sends = []
    for chunk in range(PAIRS // 2):
        at = pl.ds(2 * chunk, 2)
        for way, (own, dec, into, out, hears, tells, peer) in enumerate(ways):
            copy = push(
                out.at[at], into.at[at], send.at[way, chunk], recv.at[way, chunk], "seq", peer
            )
            sends.append((copy, tells))

            @pl.when(hears)
            def _():
                copy.wait_recv()

            @pl.when(tells)
            def _():
                for i in (2 * chunk, 2 * chunk + 1):
                    for q in range(4):
                        carried = dec[i, q, 0:1] * into[i, q].astype(F32)
                        out[i, q] = (own[i, q] + carried).astype(BF16)
                copy.start()

    for copy, tells in sends:

        @pl.when(tells)
        def _():
            copy.wait_send()


def last_kernel(
    shards, count, fold,
    hid_ref, w_ref, wr_ref, gi_ref, ddt_ref, gf_ref, heads_ref,
    gh_ref, gw_ref, gc_ref, gd_ref,
    before, after, parts, part_in, mine, chunk_in, full, total, small, small_in, small2, small2_in,
    taps, sides, zs, zr, ss, sr,
):
    seq, zero = lax.axis_index("seq"), lax.axis_index("zero")
    rows = WIDTH // shards
    fold_rows = rows // fold
    chunk = mine.shape[0] // count
    greet_all((("zero", shards), ("seq", count)))
    up = push(
        gi_ref.at[:, pl.ds(EDGE + SPAN, EDGE)], before, sides.at[0], sides.at[1], "seq",
        lax.rem(seq + 1, count),
    )
    down = push(
        gi_ref.at[:, pl.ds(0, EDGE)], after, sides.at[2], sides.at[3], "seq",
        lax.rem(seq + count - 1, count),
    )

    @pl.when(seq < count - 1)
    def _():
        up.start()

    @pl.when(seq > 0)
    def _():
        down.start()

    @pl.when(seq == 0)
    def _():
        before[...] = jnp.zeros_like(before)

    @pl.when(seq == count - 1)
    def _():
        after[...] = jnp.zeros_like(after)

    flip = mirror()
    small[...] = jnp.zeros_like(small)
    for i in range(PAIRS):
        at = slice(i * 128, i * 128 + 128)
        other = slice((PAIRS - 1 - i) * 128, (PAIRS - i) * 128)
        block = gf_ref[0, :, at] + exact(gf_ref[1, :, other], mirror(F32))
        small[KERNEL * i : KERNEL * i + KERNEL] = block[:KERNEL]
    block = gf_ref[0, :, WIDTH:] + gf_ref[1, :, WIDTH:]
    small[KERNEL * PAIRS : KERNEL * PAIRS + KERNEL] = block[:KERNEL]
    small[KERNEL * PAIRS + KERNEL : KERNEL * PAIRS + KERNEL + 2] = heads_ref[:2]
    first = []
    for k in range(1, shards):
        peer = lax.rem(zero + k, shards)
        copy = push(small, small_in.at[zero], zs.at[1, k], zr.at[1, k], "zero", peer)
        copy.start()
        first.append(copy)
    small_in[zero] = small[...]

    @pl.when(seq > 0)
    def _():
        up.wait_recv()

    @pl.when(seq < count - 1)
    def _():
        down.wait_recv()

    def own(s, at):
        top = gi_ref[s, EDGE : 2 * EDGE, at] + before[s, :, at]
        low = gi_ref[s, SPAN : SPAN + EDGE, at] + after[s, :, at]
        return jnp.concatenate([top, gi_ref[s, 2 * EDGE : SPAN, at], low], axis=0).astype(BF16)

    gps = [
        jnp.concatenate([own(s, slice(WIDTH, CHANNELS)), ddt_ref[s]], axis=1) for s in range(2)
    ]
    for i in range(PAIRS):
        at = slice(i * 128, i * 128 + 128)
        other = slice((PAIRS - 1 - i) * 128, (PAIRS - i) * 128)
        hid_flip = mm(hid_ref[:, other], flip).astype(BF16)
        total[at] = mm_tn(hid_ref[:, at], gps[0]) + mm_tn(hid_flip, gps[1])
    for z in range(shards):
        parts[z, :rows] = total[z * rows : (z + 1) * rows, :128].astype(BF16)
        folded = jnp.zeros((fold_rows, 128), F32)
        for q in range(fold):
            start = z * rows + q * fold_rows
            piece = total[start : start + fold_rows, 128:]
            folded = folded + (pltpu.roll(piece, 32 * q, 1) if q else piece)
        parts[z, rows : rows + fold_rows] = folded.astype(BF16)
        spare = parts.shape[1] - rows - fold_rows
        if spare:
            parts[z, rows + fold_rows :] = jnp.zeros((spare, 128), BF16)
    scatter = []
    for k in range(1, shards):
        peer = lax.rem(zero + k, shards)
        copy = push(parts.at[peer], part_in.at[k], zs.at[0, k], zr.at[0, k], "zero", peer)
        copy.start()
        scatter.append(copy)
    for copy in first:
        copy.wait()
    small2[...] = small_in[0]
    for z in range(1, shards):
        small2[...] += small_in[z]
    second = []
    for k in range(1, count):
        peer = lax.rem(seq + k, count)
        copy = push(small2, small2_in.at[seq], ss.at[0, k], sr.at[0, k], "seq", peer)
        copy.start()
        second.append(copy)
    small2_in[seq] = small2[...]
    for i in range(PAIRS):
        at = slice(i * 128, i * 128 + 128)
        a = (own(0, at).astype(F32) + mm_nt(gps[0], w_ref[at])).astype(BF16)
        b = (own(1, at).astype(F32) + mm_nt(gps[1], wr_ref[at])).astype(BF16)
        gh_ref[:, at] = (a.astype(F32) + b.astype(F32)).astype(BF16)
    for copy in scatter:
        copy.wait()
    summed = parts[zero].astype(F32)
    for k in range(1, shards):
        summed = summed + part_in[k].astype(F32)
    mine[...] = summed.astype(BF16)
    third = []
    for k in range(1, count):
        peer = lax.rem(seq + k, count)
        src = mine.at[pl.ds(pl.multiple_of(peer * chunk, 16), chunk)]
        copy = push(src, chunk_in.at[k], ss.at[1, k], sr.at[1, k], "seq", peer)
        copy.start()
        third.append(copy)
    for copy in third:
        copy.wait()
    here = pl.ds(pl.multiple_of(seq * chunk, 16), chunk)
    summed = mine[here].astype(F32)
    for k in range(1, count):
        summed = summed + chunk_in[k].astype(F32)
    full[here] = summed.astype(BF16)
    third = []
    for k in range(1, count):
        peer = lax.rem(seq + k, count)
        copy = push(full.at[here], full.at[here], ss.at[2, k], sr.at[2, k], "seq", peer)
        copy.start()
        third.append(copy)
    for copy in second:
        copy.wait()
    summed = small2_in[0]
    for z in range(1, count):
        summed = summed + small2_in[z]
    gd_ref[...] = summed[KERNEL * PAIRS + KERNEL : KERNEL * PAIRS + KERNEL + 2, :HEADS]
    for i in range(PAIRS + 1):
        taps[:, i * 128 : i * 128 + 128] = summed[KERNEL * i : KERNEL * i + KERNEL]
    width = gc_ref.shape[1]
    for z in range(shards):

        @pl.when(zero == z)
        def _():
            gc_ref[...] = taps[:, z * width : (z + 1) * width]

    for copy in third:
        copy.wait()

    @pl.when(seq < count - 1)
    def _():
        up.wait_send()

    @pl.when(seq > 0)
    def _():
        down.wait_send()

    gw_ref[:, :128] = full[:rows].astype(F32)
    tail = full[rows : rows + fold_rows].astype(F32)
    for q in range(fold):
        gw_ref[q * fold_rows : (q + 1) * fold_rows, 128:] = tail[:, 32 * q : 32 * q + HEADS]


def call(body, outs, scratch=(), sems=(), number=None):
    return pl.pallas_call(
        body,
        out_shape=[jax.ShapeDtypeStruct(s, t) for s, t in outs],
        scratch_shapes=[pltpu.VMEM(s, t) for s, t in scratch]
        + [pltpu.SemaphoreType.DMA(s) for s in sems],
        compiler_params=pltpu.CompilerParams(
            vmem_limit_bytes=48 * 1024 * 1024,
            collective_id=number,
            has_side_effects=number is not None,
        ),
    )


SQ4 = (4, 128, 128)
SQ2 = (2, 128, 128)


def per_device(hidden, grad_out, w_proj, conv_w, a_log, dt_bias):
    hid, go = hidden[0], grad_out[0]
    assert hidden.shape[:2] == (1, SPAN)
    count, shards = lax.axis_size("seq"), lax.axis_size("zero")
    rows = WIDTH // shards
    part = CHANNELS // shards
    alog = jnp.pad(a_log, (0, 128 - HEADS))[None]
    bias = jnp.pad(dt_bias, (0, 128 - HEADS))[None]
    x_ext, w_full, filters = call(
        functools.partial(gather_kernel, shards, count),
        [((EXT, WIDTH), BF16), ((WIDTH, 256), BF16), ((8, CHANNELS), F32)],
        [
            ((shards,) + w_proj.shape, BF16), ((8, part), F32), ((shards, 8, part), F32),
            ((2 * EDGE, WIDTH), BF16), ((2 * EDGE, WIDTH), BF16),
        ],
        [(shards, 2), (shards, 2), (4,)],
        0,
    )(hid, w_proj, conv_w)
    pieces = (PAIRS, 4, STATE, 128)
    own_up, own_down, dec_up, dec_down, w_rev, bcx, dtx, within = call(
        first_kernel,
        [
            (pieces, F32), (pieces, F32), ((PAIRS, 4, 8, 128), F32), ((PAIRS, 4, 8, 128), F32),
            ((WIDTH, 256), BF16), ((2, EXT, 128), F32), (SQ2, F32), (SQ4, F32),
        ],
        [(SQ4, F32)] * 3,
    )(x_ext, go, w_full, filters, alog, bias)
    in_up, in_down = call(
        functools.partial(chain_kernel, count),
        [(pieces, BF16), (pieces, BF16)],
        [(pieces, BF16), (pieces, BF16)],
        [(2, PAIRS // 2), (2, PAIRS // 2)],
        1,
    )(own_up, own_down, dec_up, dec_down)
    output, gi, gf, ddt, heads = call(
        main_kernel,
        [
            ((SPAN, WIDTH), BF16), ((2, EXT, CHANNELS), F32), ((2, 8, CHANNELS), F32),
            (SQ2, BF16), ((8, 128), F32),
        ],
        [
            (s, F32)
            for s in (
                SQ4, SQ4, SQ4, SQ4, SQ2, SQ4, SQ4, (4, 128, STATE), (4, 128, STATE), SQ4, SQ4,
                SQ2, SQ2, (4, 2, 128, STATE),
            )
        ],
    )(x_ext, go, filters, alog, bcx, dtx, within, in_up, in_down)
    fold = 4 if rows % 64 == 0 else 1
    step = 16 * count
    padded = -(-(rows + rows // fold) // step) * step
    lines = 48
    grad_hidden, share_w, share_c, grad_heads = call(
        functools.partial(last_kernel, shards, count, fold),
        [
            ((SPAN, WIDTH), BF16), (w_proj.shape, F32), ((KERNEL, part), F32), ((2, HEADS), F32),
        ],
        [
            ((2, EDGE, CHANNELS), F32), ((2, EDGE, CHANNELS), F32),
            ((shards, padded, 128), BF16), ((shards, padded, 128), BF16),
            ((padded, 128), BF16), ((count, padded // count, 128), BF16), ((padded, 128), BF16),
            ((WIDTH, 256), F32),
            ((lines, 128), F32), ((shards, lines, 128), F32),
            ((lines, 128), F32), ((count, lines, 128), F32), ((KERNEL, CHANNELS), F32),
        ],
        [(4,), (2, shards), (2, shards), (3, count), (3, count)],
        2,
    )(hid, w_full, w_rev, gi, ddt, gf, heads)
    return (output[None], grad_hidden[None], share_w, share_c, grad_heads)


def solution(mesh):
    return jax.shard_map(
        per_device,
        mesh=mesh,
        in_specs=(
            P(("grp", "zero"), "seq", None),
            P(("grp", "zero"), "seq", None),
            P("zero", None),
            P(None, "zero"),
            P(),
            P(),
        ),
        out_specs=(
            P(("grp", "zero"), "seq", None),
            P(("grp", "zero"), "seq", None),
            P(("grp", "zero"), None),
            P("grp", "zero"),
            P("grp", None),
        ),
        check_vma=False,
    )
```
